1024 devices in a mesh: gx: 32 (over z_lo, core), gy: 32 (over x, y, z_hi).
Axes of the slice: x: 4, y: 4, z: 32 (z_hi: 2, z_lo: 16; z = z_hi * 16 + z_lo), core: 2. Of those that a mesh axis runs over, the one named last changes fastest.
Arguments:
- adjoint_fields: float32 [6, 256, 1024, 128], P(None, 'gx', 'gy'), may hold values from -6 to 6
- forward_e: bfloat16 [4, 3, 256, 1024, 128], P(None, None, 'gx', 'gy'), may hold values from -6 to 6
- permittivity: float32 [256, 1024, 128], P('gx', 'gy'), may hold values from 1 to 12
- design_mask: int32 [256, 1024, 128], P('gx', 'gy'), may hold values 0 or 1
- band_offsets: int32 [9], replicated, may hold values from -64 to 64, as said below
- filter_taps: float32 [9], replicated, may hold values from 0.05 to 0.5
Outputs:
- filtered: float32 [256, 1024, 128], P('gx', 'gy')
- adjoint_e: float32 [3, 256, 1024, 128], P(None, 'gx', 'gy')
The draws below stay inside these ranges and needn't reach their ends.
Inputs may be any that keep to these rules, and one draw needn't show every extreme that they name: `band_offsets`: the offsets are distinct; both -64 and 64 occur.
All inputs are finite; a program needn't handle non-finite values. No bound on the sum of `design_mask` on one device may be relied on, other than what follows from the above.
Results may differ from the reference program's by a relative error of at most 0.0003.
Values sent between devices are 32-bit elements; how exact they have to be, the bound alone decides.
A program may use at most 32 MiB of HBM per device.

```python
import math
import jax
import jax.numpy as jnp
from jax import lax

NZ = 128
ITERS = 4
BAND = 9
NX = 256
NY = 1024
REACH = 64


def draw_band_offsets(key, part):
    inner = jax.random.permutation(key, 2 * REACH - 1)[:BAND - 2].astype(jnp.int32) - (REACH - 1)
    ends = jnp.array([-REACH, REACH], jnp.int32)
    return jnp.concatenate([ends, inner])


def plant(result, stream_key, low, high):
    extent = result.shape
    index_at = [jax.random.randint(jax.random.fold_in(stream_key, axis), (), 0, extent[axis]) for axis in range(len(extent))]
    result = result.at[tuple(index_at)].set(low)
    longest = extent.index(max(extent))
    index_at[longest] = (index_at[longest] + 1) % extent[longest]
    return result.at[tuple(index_at)].set(high)


def block_scale(own_key, dims, pieces, least, top_value):
    factor_of, own = 1.0, jax.random.fold_in(own_key, 6)
    for position, parts in pieces:
        steps = jnp.exp(jax.random.uniform(jax.random.fold_in(own, position), (parts,), jnp.float32, least / len(pieces), top_value / len(pieces)))
        factor_of = factor_of * jnp.repeat(steps, dims[position] // parts).reshape([-1 if axis == position else 1 for axis in range(len(dims))])
    return factor_of


def noise(own_key, dims, deviation, bound, pieces=(), kind=jnp.bfloat16):
    drawn = jax.random.normal(own_key, dims, jnp.float32) * deviation
    if len(pieces) > 0:
        drawn = block_scale(own_key, dims, pieces, -0.22, 0.18) * drawn
    return jnp.clip(drawn, min=-bound, max=bound).astype(kind)


def setup_inputs(seed: int = 0) -> dict:
    seeds = jax.random.split(jax.random.key(seed), 7)
    adjoint_fields = noise(seeds[0], (6, NX, NY, NZ), 1.0, 6.0, ((1, 32), (2, 32)), jnp.float32)
    forward_e = noise(seeds[1], (ITERS, 3, NX, NY, NZ), 1.0, 6.0, ((2, 32), (3, 32)))
    permittivity = jnp.clip(1.0 + 11.0 * jax.random.uniform(seeds[2], (NX, NY, NZ), jnp.float32) ** block_scale(seeds[2], (NX, NY, NZ), ((0, 32), (1, 32)), -0.2, 0.2), 1.0, 12.0)
    design_mask = plant((jax.random.randint(seeds[3], (NX, NY, NZ), 0, 4) < 3).astype(jnp.int32), jax.random.fold_in(seeds[3], 1), 0, 1)
    band_offsets = draw_band_offsets(jax.random.fold_in(seeds[6], 71), 0)
    filter_taps = jnp.clip(jnp.exp(jax.random.uniform(seeds[5], (BAND,), jnp.float32, math.log(0.05), math.log(0.5))), 0.05, 0.5)
    return {"adjoint_fields": adjoint_fields, "forward_e": forward_e, "permittivity": permittivity, "design_mask": design_mask, "band_offsets": band_offsets, "filter_taps": filter_taps}


courant = 0.5


def forward_diff(quantity, along):
    widths = [(0, 0)] * quantity.ndim
    widths[along] = (0, 1)
    padded = jnp.pad(quantity, widths)
    return lax.slice_in_dim(padded, 1, quantity.shape[along] + 1, axis=along) - quantity


def backward_diff(quantity, along):
    widths = [(0, 0)] * quantity.ndim
    widths[along] = (1, 0)
    padded = jnp.pad(quantity, widths)
    return quantity - lax.slice_in_dim(padded, 0, quantity.shape[along], axis=along)


def reference(adjoint_fields, forward_e, permittivity, design_mask, band_offsets, filter_taps):
    elec_x, elec_y, elec_z = adjoint_fields[0], adjoint_fields[1], adjoint_fields[2]
    magn_x, magn_y, magn_z = adjoint_fields[3], adjoint_fields[4], adjoint_fields[5]
    factor = courant / permittivity
    gradient = jnp.zeros(permittivity.shape, jnp.float32)
    for turn in range(ITERS):
        magn_x = magn_x - courant * (forward_diff(elec_z, 1) - forward_diff(elec_y, 2))
        magn_y = magn_y - courant * (forward_diff(elec_x, 2) - forward_diff(elec_z, 0))
        magn_z = magn_z - courant * (forward_diff(elec_y, 0) - forward_diff(elec_x, 1))
        elec_x = elec_x + factor * (backward_diff(magn_z, 1) - backward_diff(magn_y, 2))
        elec_y = elec_y + factor * (backward_diff(magn_x, 2) - backward_diff(magn_z, 0))
        elec_z = elec_z + factor * (backward_diff(magn_y, 0) - backward_diff(magn_x, 1))
        stored = forward_e[turn].astype(jnp.float32)
        gradient = gradient + (stored[0] * elec_x + stored[1] * elec_y + stored[2] * elec_z)
    masked = gradient * design_mask.astype(jnp.float32)
    total = masked.shape[0]
    padded = jnp.pad(masked, ((REACH, REACH), (0, 0), (0, 0)))
    filtered = jnp.zeros(masked.shape, jnp.float32)
    for index in range(BAND):
        start = (REACH + band_offsets[index]).astype(jnp.int32)
        filtered = filtered + filter_taps[index] * lax.dynamic_slice_in_dim(padded, start, total, 0)
    return filtered, jnp.stack([elec_x, elec_y, elec_z])
```

```python
import functools

import jax
import jax.numpy as jnp
from jax import lax
from jax.experimental import pallas as pl
from jax.experimental.pallas import tpu as pltpu
from jax.sharding import PartitionSpec as P

ITERS = 4
BAND = 9
REACH = 64
courant = 0.5

MESH = pl.DeviceIdType.MESH
F32 = jnp.float32
ROWS = 8
EDGE = 4
WIDE = ROWS + 2 * EDGE
NY = 32
NZ = 128
LEFT_BOUND = (0, 2, 3, 4, 5)
RIGHT_BOUND = (1, 6, 7, 8, 9)
MESSAGES = 10
CHIPS = 4


def kernel(
    nx, ny,
    fields_hbm, stored_hbm, perm_hbm, mask_hbm, off_ref, tap_ref,
    filt_ref, final_ref,
    F, FE, PV, MV, G, SB, RB, D, CS, GS, WA, WB,
    load_sem, x_send, x_recv, far_send, far_recv, fwd_send, fwd_recv,
    za_send, za_recv, pa_send, pa_recv, zb_send, zb_recv, pb_send, pb_recv,
):
    gx, gy = lax.axis_index("gx"), lax.axis_index("gy")
    core, chip, chips = gx % 2, gx // 2, nx // 2
    has_left, has_right = gx > 0, gx < nx - 1
    has_below, has_above = gy > 0, gy < ny - 1

    loads = [
        pltpu.make_async_copy(fields_hbm, F.at[pl.ds(0, 6), pl.ds(EDGE, ROWS)], load_sem.at[0]),
        pltpu.make_async_copy(perm_hbm, PV, load_sem.at[1]),
        pltpu.make_async_copy(stored_hbm, FE, load_sem.at[2]),
        pltpu.make_async_copy(mask_hbm, MV, load_sem.at[3]),
    ]
    for load in loads:
        load.start()

    def clear(ref, length):
        @pl.loop(0, length)
        def _(i):
            ref[i] = jnp.zeros(ref.shape[1:], F32)

    RB[...] = jnp.zeros(RB.shape, F32)

    @pl.when(jnp.logical_not(has_left))
    def _():
        for k in range(7):
            for r in range(EDGE):
                F[k, r] = jnp.zeros((NY, NZ), F32)

    @pl.when(jnp.logical_not(has_right))
    def _():
        for k in range(7):
            for r in range(EDGE):
                F[k, EDGE + ROWS + r] = jnp.zeros((NY, NZ), F32)

    @pl.when((gx < ROWS) | (gx >= nx - ROWS))
    def _():
        clear(WA, 17 * ROWS)
        clear(WB, 17 * ROWS)

    barrier = pltpu.get_barrier_semaphore()

    def greet(condition, where):
        @pl.when(condition)
        def _():
            pl.semaphore_signal(barrier, inc=1, device_id=where, device_id_type=MESH)

    up_chip, down_chip = chip < chips - 1, chip > 0
    greet(has_below, {"gy": gy - 1})
    greet(has_above, {"gy": gy + 1})
    greet(has_left, {"gx": gx - 1})
    greet(has_right, {"gx": gx + 1})
    greet(down_chip, {"gx": gx - 2})
    greet(up_chip, {"gx": gx + 2})

    iy = lax.broadcasted_iota(jnp.int32, (NY, NZ), 0)
    iz = lax.broadcasted_iota(jnp.int32, (NY, NZ), 1)
    sub = lax.broadcasted_iota(jnp.int32, (8, NZ), 0)
    lane = lax.broadcasted_iota(jnp.int32, (8, NZ), 1)

    loads[0].wait()
    loads[1].wait()

    @pl.loop(0, ROWS)
    def _(r):
        c = courant / PV[r]
        F[6, EDGE + r] = c
        row = pl.ds(r + 8, 1)
        SB[0, 0, row] = c[0:1]
        SB[0, 1, row] = c[1:2]
        SB[1, 0, row] = c[31:32]
        SB[1, 1, row] = c[30:31]

    def level0(x):
        row = pl.ds(x + 4, 1)
        SB[2, 0, row] = F[0, x, pl.ds(0, 1), :]
        SB[2, 1, row] = F[2, x, pl.ds(0, 1), :]

    @pl.loop(EDGE, EDGE + ROWS)
    def _(x):
        level0(x)

    def count(condition):
        return jnp.where(condition, 1, 0)

    pl.semaphore_wait(
        barrier,
        count(has_below) + count(has_above) + count(has_left) + count(has_right) + count(down_chip) + count(up_chip),
    )

    def to_left():
        return pltpu.make_async_remote_copy(
            src_ref=F.at[:, pl.ds(EDGE, EDGE)], dst_ref=F.at[:, pl.ds(EDGE + ROWS, EDGE)],
            send_sem=x_send.at[0], recv_sem=x_recv.at[0], device_id={"gx": gx - 1}, device_id_type=MESH,
        )

    def to_right():
        return pltpu.make_async_remote_copy(
            src_ref=F.at[:, pl.ds(ROWS, EDGE)], dst_ref=F.at[:, pl.ds(0, EDGE)],
            send_sem=x_send.at[1], recv_sem=x_recv.at[1], device_id={"gx": gx + 1}, device_id_type=MESH,
        )

    pl.when(has_left)(lambda: to_left().start())
    pl.when(has_right)(lambda: to_right().start())

    middle = pl.ds(8, 8)

    def far(m):
        where = {"gy": gy - 1} if m in LEFT_BOUND else {"gy": gy + 1}
        return pltpu.make_async_remote_copy(
            src_ref=SB.at[m, :, middle], dst_ref=RB.at[m, :, middle],
            send_sem=far_send.at[m], recv_sem=far_recv.at[m], device_id=where, device_id_type=MESH,
        )

    def sends(m):
        return has_below if m in LEFT_BOUND else has_above

    def receives(m):
        return has_above if m in LEFT_BOUND else has_below

    def post(m):
        pl.when(sends(m))(lambda: far(m).start())

    post(0)
    post(1)
    post(2)

    pl.when(has_right)(lambda: to_left().wait_recv())
    pl.when(has_left)(lambda: to_right().wait_recv())
    pl.when(has_left)(lambda: to_left().wait_send())
    pl.when(has_right)(lambda: to_right().wait_send())

    for x in (*range(0, EDGE), *range(EDGE + ROWS, WIDE)):
        level0(x)
    loads[2].wait()
    loads[3].wait()

    def half(x):
        outside = (jnp.logical_not(has_left) & (x < EDGE)) | (jnp.logical_not(has_right) & (x >= EDGE + ROWS))
        return jnp.where(outside, 0.0, courant).astype(F32)

    def next_y(v):
        return jnp.where(iy < NY - 1, pltpu.roll(v, NY - 1, 0), 0.0)

    def last_y(v):
        return jnp.where(iy > 0, pltpu.roll(v, 1, 0), 0.0)

    def next_z(v):
        return jnp.where(iz < NZ - 1, pltpu.roll(v, NZ - 1, 1), 0.0)

    def last_z(v):
        return jnp.where(iz > 0, pltpu.roll(v, 1, 1), 0.0)

    def magnetic(x, step):
        s = half(x)
        ex, ey, ez = F[0, x], F[1, x], F[2, x]
        hx = F[3, x] - s * ((next_y(ez) - ez) - (next_z(ey) - ey))
        hy = F[4, x] - s * ((next_z(ex) - ex) - (F[2, x + 1] - ez))
        hz = F[5, x] - s * ((F[1, x + 1] - ey) - (next_y(ex) - ex))
        F[3, x], F[4, x], F[5, x] = hx, hy, hz
        row = pl.ds(x + 4, 1)
        SB[6 + step, 0, row] = hx[NY - 1 : NY]
        SB[6 + step, 1, row] = hz[NY - 1 : NY]
        return ex, ey, ez, hx, hy, hz

    def both(x, step, graded):
        ex, ey, ez, hx, hy, hz = magnetic(x, step)
        c = F[6, x]
        ex = ex + c * ((hz - last_y(hz)) - (hy - last_z(hy)))
        ey = ey + c * ((hx - last_z(hx)) - (hz - F[5, x - 1]))
        ez = ez + c * ((hy - F[4, x - 1]) - (hx - last_y(hx)))
        F[0, x], F[1, x], F[2, x] = ex, ey, ez
        if step < ITERS - 1:
            row = pl.ds(x + 4, 1)
            SB[3 + step, 0, row] = ex[0:1]
            SB[3 + step, 1, row] = ez[0:1]
        if graded:
            r = x - EDGE
            g = FE[step, 0, r].astype(F32) * ex + FE[step, 1, r].astype(F32) * ey + FE[step, 2, r].astype(F32) * ez
            G[r] = g if step == 0 else G[r] + g

    for step in range(ITERS):
        magnetic(step, step)
        lax.fori_loop(step + 1, EDGE, lambda x, _: (both(x, step, False), 0)[1], 0)
        lax.fori_loop(EDGE, EDGE + ROWS, lambda x, _: (both(x, step, True), 0)[1], 0)
        lax.fori_loop(EDGE + ROWS, WIDE - 1 - step, lambda x, _: (both(x, step, False), 0)[1], 0)
        post(6 + step)
        if step < ITERS - 1:
            post(3 + step)

    lower = sub < 4

    def gather(W, z_send, z_recv, p_send, p_recv):
        def slot(s):
            return W.at[pl.ds(ROWS * s, ROWS)]

        def relay(way, k):
            sign = -1 if way == 0 else 1
            return pltpu.make_async_remote_copy(
                src_ref=slot(8 + sign * 2 * (k - 1)), dst_ref=slot(8 + sign * 2 * k),
                send_sem=z_send.at[way, k - 1], recv_sem=z_recv.at[way, k - 1],
                device_id={"gx": gx - 2 * sign}, device_id_type=MESH,
            )

        def exists(way, k):
            return chip >= k if way == 0 else chip + k <= chips - 1

        def relays(way, k):
            onward = up_chip if way == 0 else down_chip
            return onward if k == 1 else onward & exists(way, k - 1)

        def across(way, k):
            sign = -1 if way == 0 else 1
            s = 8 + sign * 2 * k
            i = s // 2 - 1 + core
            return pltpu.make_async_remote_copy(
                src_ref=slot(s), dst_ref=slot(2 * i + 1),
                send_sem=p_send.at[s // 2], recv_sem=p_recv.at[i],
                device_id={"gx": gx + 1 - 2 * core}, device_id_type=MESH,
            )

        def crosses(way, k):
            if k == 0:
                return None
            known = exists(way, k)
            if k == CHIPS:
                known = known & (core == 1 if way == 0 else core == 0)
            return known

        def begin():
            pl.when(relays(0, 1))(lambda: relay(0, 1).start())
            pl.when(relays(1, 1))(lambda: relay(1, 1).start())
            across(0, 0).start()

        def step(k):
            for way in (0, 1):
                pl.when(exists(way, k))(functools.partial(lambda w: relay(w, k).wait_recv(), way))
                if k < CHIPS:
                    pl.when(relays(way, k + 1))(functools.partial(lambda w: relay(w, k + 1).start(), way))
                pl.when(crosses(way, k))(functools.partial(lambda w: across(w, k).start(), way))

        def finish():
            for i in range(8):
                other = gx + 2 * i + 1 - 8
                copy = pltpu.make_async_remote_copy(
                    src_ref=slot(2 * i + 1), dst_ref=slot(2 * i + 1),
                    send_sem=p_send.at[0], recv_sem=p_recv.at[i],
                    device_id={"gx": gx + 1 - 2 * core}, device_id_type=MESH,
                )
                pl.when((other >= 0) & (other < nx))(copy.wait_recv)

        def drain():
            across(0, 0).wait_send()
            for k in range(1, CHIPS + 1):
                for way in (0, 1):
                    pl.when(relays(way, k))(functools.partial(lambda w, j: relay(w, j).wait_send(), way, k))
                    pl.when(crosses(way, k))(functools.partial(lambda w, j: across(w, j).wait_send(), way, k))

        return begin, step, finish, drain

    begin_a, step_a, finish_a, drain_a = gather(WA, za_send, za_recv, pa_send, pa_recv)
    begin_b, step_b, finish_b, drain_b = gather(WB, zb_send, zb_recv, pb_send, pb_recv)

    @pl.loop(0, ROWS)
    def _(r):
        m = G[r] * MV[r].astype(F32)
        WA[8 * ROWS + r, pl.ds(0, 16), :] = m[8:24]
        WA[8 * ROWS + r, pl.ds(16, 8), :] = jnp.where(lower, m[24:32], m[0:8])

    begin_a()
    for k in range(1, CHIPS + 1):
        step_a(k)

    def forward(m, way):
        tile = 2 if way == 0 else 0
        where = {"gx": gx - 1} if way == 0 else {"gx": gx + 1}
        return pltpu.make_async_remote_copy(
            src_ref=RB.at[m, :, middle], dst_ref=RB.at[m, :, pl.ds(8 * tile, 8)],
            send_sem=fwd_send.at[m, way], recv_sem=fwd_recv.at[m, way], device_id=where, device_id_type=MESH,
        )

    order = (0, 1, 2, 6, 3, 7, 4, 8, 5, 9)
    for m in order:
        pl.when(receives(m))(functools.partial(lambda i: far(i).wait_recv(), m))
        pl.when(receives(m) & has_left)(functools.partial(lambda i: forward(i, 0).start(), m))
        pl.when(receives(m) & has_right)(functools.partial(lambda i: forward(i, 1).start(), m))

    for k in range(6):
        for side in range(2):
            D[side, k] = jnp.zeros((WIDE, 8, NZ), F32)

    def arrived(m):
        pl.when(receives(m) & has_right)(functools.partial(lambda i: forward(i, 0).wait_recv(), m))
        pl.when(receives(m) & has_left)(functools.partial(lambda i: forward(i, 1).wait_recv(), m))

    for m in order:
        arrived(m)

    @pl.loop(0, WIDE)
    def _(x):
        row = pl.ds(x + 4, 1)
        c = F[6, x]
        near, next_near = RB[1, 0, row], RB[1, 1, row]
        CS[0, x] = jnp.where(lower, c[0:8], jnp.where(sub == 7, near, jnp.where(sub == 6, next_near, 0.0)))
        near, next_near = RB[0, 0, row], RB[0, 1, row]
        CS[1, x] = jnp.where(lower, jnp.where(sub == 0, near, jnp.where(sub == 1, next_near, 0.0)), c[24:32])

    inflow = jnp.where(has_below, 1.0, 0.0).astype(F32)

    def next_s(v, trace):
        return pltpu.roll(v, 7, 0) + jnp.where(sub == 7, trace, 0.0)

    def last_s(v, trace):
        return pltpu.roll(v, 1, 0) + jnp.where(sub == 0, trace, 0.0)

    def up(v):
        return jnp.where(lane < NZ - 1, pltpu.roll(v, NZ - 1, 1), 0.0)

    def down(v):
        return jnp.where(lane > 0, pltpu.roll(v, 1, 1), 0.0)

    def strip_magnetic(side, x, step):
        s = half(x)
        row = pl.ds(x + 4, 1)
        if side == 0:
            tx, tz = SB[2 + step, 0, row] * inflow, SB[2 + step, 1, row] * inflow
        else:
            tx, tz = RB[2 + step, 0, row], RB[2 + step, 1, row]
        ex, ey, ez = D[side, 0, x], D[side, 1, x], D[side, 2, x]
        hx = D[side, 3, x] - s * ((next_s(ez, tz) - ez) - (up(ey) - ey))
        hy = D[side, 4, x] - s * ((up(ex) - ex) - (D[side, 2, x + 1] - ez))
        hz = D[side, 5, x] - s * ((D[side, 1, x + 1] - ey) - (next_s(ex, tx) - ex))
        D[side, 3, x], D[side, 4, x], D[side, 5, x] = hx, hy, hz
        return ex, ey, ez, hx, hy, hz

    def strip_both(side, x, step, graded):
        ex, ey, ez, hx, hy, hz = strip_magnetic(side, x, step)
        row = pl.ds(x + 4, 1)
        planes = RB if side == 0 else SB
        tx, tz = planes[6 + step, 0, row], planes[6 + step, 1, row]
        c = CS[side, x]
        ex = ex + c * ((hz - last_s(hz, tz)) - (hy - down(hy)))
        ey = ey + c * ((hx - down(hx)) - (hz - D[side, 5, x - 1]))
        ez = ez + c * ((hy - D[side, 4, x - 1]) - (hx - last_s(hx, tx)))
        D[side, 0, x], D[side, 1, x], D[side, 2, x] = ex, ey, ez
        if graded:
            r = x - EDGE
            if side == 0:
                stored = [FE[step, k, r, pl.ds(0, 16), :].astype(F32)[0:8] for k in range(3)]
            else:
                stored = [FE[step, k, r, pl.ds(16, 16), :].astype(F32)[8:16] for k in range(3)]
            g = stored[0] * ex + stored[1] * ey + stored[2] * ez
            GS[side, r] = g if step == 0 else GS[side, r] + g

    def strips(x, step, graded):
        strip_both(0, x, step, graded)
        strip_both(1, x, step, graded)
        return 0

    for step in range(ITERS):
        strip_magnetic(0, step, step)
        strip_magnetic(1, step, step)
        lax.fori_loop(step + 1, EDGE, lambda x, _: strips(x, step, False), 0)
        lax.fori_loop(EDGE, EDGE + ROWS, lambda x, _: strips(x, step, True), 0)
        lax.fori_loop(EDGE + ROWS, WIDE - 1 - step, lambda x, _: strips(x, step, False), 0)

    @pl.loop(0, ROWS)
    def _(r):
        g = jnp.where(lower, G[r, pl.ds(0, 8), :] + GS[0, r], G[r, pl.ds(24, 8), :] + GS[1, r])
        mask = jnp.where(lower, MV[r, pl.ds(0, 8), :], MV[r, pl.ds(24, 8), :])
        WB[8 * ROWS + r] = g * mask.astype(F32)

    begin_b()

    @pl.loop(0, ROWS)
    def _(r):
        x = r + EDGE
        for k in range(3):
            e = F[k, x]
            final_ref[k, r, pl.ds(8, 16), :] = e[8:24]
            final_ref[k, r, pl.ds(0, 8), :] = e[0:8] + jnp.where(lower, D[0, k, x], 0.0)
            final_ref[k, r, pl.ds(24, 8), :] = e[24:32] + jnp.where(lower, 0.0, D[1, k, x])

    finish_a()
    for k in range(1, CHIPS + 1):
        step_b(k)
    finish_b()

    taps = [tap_ref[b] for b in range(BAND)]
    starts = [off_ref[b] + REACH for b in range(BAND)]

    @pl.loop(0, ROWS)
    def _(r):
        wide, thin = taps[0] * WA[starts[0] + r], taps[0] * WB[starts[0] + r]
        for b in range(1, BAND):
            wide = wide + taps[b] * WA[starts[b] + r]
            thin = thin + taps[b] * WB[starts[b] + r]
        mixed = wide[16:24]
        filt_ref[r, pl.ds(8, 16), :] = wide[0:16]
        filt_ref[r, pl.ds(0, 8), :] = jnp.where(lower, thin, mixed)
        filt_ref[r, pl.ds(24, 8), :] = jnp.where(lower, mixed, thin)

    for m in range(MESSAGES):
        pl.when(sends(m))(functools.partial(lambda i: far(i).wait_send(), m))
        pl.when(receives(m) & has_left)(functools.partial(lambda i: forward(i, 0).wait_send(), m))
        pl.when(receives(m) & has_right)(functools.partial(lambda i: forward(i, 1).wait_send(), m))
    drain_a()
    drain_b()


def solution(mesh):
    nx, ny = mesh.shape["gx"], mesh.shape["gy"]

    def shards(adjoint_fields, forward_e, permittivity, design_mask, band_offsets, filter_taps):
        dma = pltpu.SemaphoreType.DMA
        hbm, vmem, smem = (pl.BlockSpec(memory_space=s) for s in (pl.ANY, pltpu.VMEM, pltpu.SMEM))
        return pl.pallas_call(
            functools.partial(kernel, nx, ny),
            out_shape=(
                jax.ShapeDtypeStruct((ROWS, NY, NZ), F32),
                jax.ShapeDtypeStruct((3, ROWS, NY, NZ), F32),
            ),
            in_specs=[hbm, hbm, hbm, hbm, smem, smem],
            out_specs=(vmem, vmem),
            scratch_shapes=[
                pltpu.VMEM((7, WIDE, NY, NZ), F32),
                pltpu.VMEM((ITERS, 3, ROWS, NY, NZ), jnp.bfloat16),
                pltpu.VMEM((ROWS, NY, NZ), F32),
                pltpu.VMEM((ROWS, NY, NZ), jnp.int32),
                pltpu.VMEM((ROWS, NY, NZ), F32),
                pltpu.VMEM((MESSAGES, 2, 24, NZ), F32),
                pltpu.VMEM((MESSAGES, 2, 24, NZ), F32),
                pltpu.VMEM((2, 6, WIDE, 8, NZ), F32),
                pltpu.VMEM((2, WIDE, 8, NZ), F32),
                pltpu.VMEM((2, ROWS, 8, NZ), F32),
                pltpu.VMEM((17 * ROWS, 24, NZ), F32),
                pltpu.VMEM((17 * ROWS, 8, NZ), F32),
                dma((4,)), dma((2,)), dma((2,)),
                dma((MESSAGES,)), dma((MESSAGES,)), dma((MESSAGES, 2)), dma((MESSAGES, 2)),
                dma((2, CHIPS)), dma((2, CHIPS)), dma((9,)), dma((8,)),
                dma((2, CHIPS)), dma((2, CHIPS)), dma((9,)), dma((8,)),
            ],
            compiler_params=pltpu.CompilerParams(collective_id=0, has_side_effects=True),
            name="adjoint_yee_filter",
        )(adjoint_fields, forward_e, permittivity, design_mask, band_offsets, filter_taps)

    return jax.shard_map(
        shards,
        mesh=mesh,
        in_specs=(
            P(None, "gx", "gy", None),
            P(None, None, "gx", "gy", None),
            P("gx", "gy", None),
            P("gx", "gy", None),
            P(),
            P(),
        ),
        out_specs=(P("gx", "gy", None), P(None, "gx", "gy", None)),
        check_vma=False,
    )
```

```python
import functools

import jax
import jax.numpy as jnp
from jax import lax
from jax.experimental import pallas as pl
from jax.experimental.pallas import tpu as pltpu
from jax.sharding import PartitionSpec as P

ITERS = 4
BAND = 9
REACH = 64
courant = 0.5

MESH = pl.DeviceIdType.MESH
F32 = jnp.float32
ROWS = 8
EDGE = 4
WIDE = ROWS + 2 * EDGE
NY = 32
NZ = 128
LEFT_BOUND = (0, 2, 3, 4, 5)
RIGHT_BOUND = (1, 6, 7, 8, 9)
MESSAGES = 10
CHIPS = 4


def kernel(
    nx, ny,
    fields_hbm, stored_hbm, perm_hbm, mask_hbm, off_ref, tap_ref,
    filt_ref, final_ref,
    F, FE, PV, MV, G, SB, RB, T, D, CS, GS, WA, WB,
    load_sem, x_send, x_recv, far_send, far_recv, fwd_send, fwd_recv,
    za_send, za_recv, pa_send, pa_recv, zb_send, zb_recv, pb_send, pb_recv,
):
    gx, gy = lax.axis_index("gx"), lax.axis_index("gy")
    core, chip, chips = gx % 2, gx // 2, nx // 2
    has_left, has_right = gx > 0, gx < nx - 1
    has_below, has_above = gy > 0, gy < ny - 1

    loads = [
        pltpu.make_async_copy(fields_hbm, F.at[pl.ds(0, 6), pl.ds(EDGE, ROWS)], load_sem.at[0]),
        pltpu.make_async_copy(perm_hbm, PV, load_sem.at[1]),
        pltpu.make_async_copy(stored_hbm, FE, load_sem.at[2]),
        pltpu.make_async_copy(mask_hbm, MV, load_sem.at[3]),
    ]
    for load in loads:
        load.start()

    def clear(ref, length):
        @pl.loop(0, length)
        def _(i):
            ref[i] = jnp.zeros(ref.shape[1:], F32)

    RB[...] = jnp.zeros(RB.shape, F32)

    @pl.when(jnp.logical_not(has_left))
    def _():
        for k in range(7):
            for r in range(EDGE):
                F[k, r] = jnp.zeros((NY, NZ), F32)

    @pl.when(jnp.logical_not(has_right))
    def _():
        for k in range(7):
            for r in range(EDGE):
                F[k, EDGE + ROWS + r] = jnp.zeros((NY, NZ), F32)

    @pl.when((gx < ROWS) | (gx >= nx - ROWS))
    def _():
        clear(WA, 17 * ROWS)
        clear(WB, 17 * ROWS)

    barrier = pltpu.get_barrier_semaphore()

    def greet(condition, where):
        @pl.when(condition)
        def _():
            pl.semaphore_signal(barrier, inc=1, device_id=where, device_id_type=MESH)

    def chip_at(way, k):
        return chip >= k if way == 0 else chip + k <= chips - 1

    up_chip, down_chip = chip_at(1, 1), chip_at(0, 1)
    greet(has_below, {"gy": gy - 1})
    greet(has_above, {"gy": gy + 1})
    greet(has_left, {"gx": gx - 1})
    greet(has_right, {"gx": gx + 1})
    for k in range(1, CHIPS + 1):
        greet(chip_at(0, k), {"gx": gx - 2 * k})
        greet(chip_at(1, k), {"gx": gx + 2 * k})

    iy = lax.broadcasted_iota(jnp.int32, (NY, NZ), 0)
    iz = lax.broadcasted_iota(jnp.int32, (NY, NZ), 1)
    sub = lax.broadcasted_iota(jnp.int32, (8, NZ), 0)
    lane = lax.broadcasted_iota(jnp.int32, (8, NZ), 1)

    loads[0].wait()
    loads[1].wait()

    @pl.loop(0, ROWS)
    def _(r):
        c = courant / PV[r]
        F[6, EDGE + r] = c
        row = pl.ds(r + 8, 1)
        SB[0, 0, row] = c[0:1]
        SB[0, 1, row] = c[1:2]
        SB[1, 0, row] = c[31:32]
        SB[1, 1, row] = c[30:31]

    def level0(x):
        row = pl.ds(x + 4, 1)
        SB[2, 0, row] = F[0, x, pl.ds(0, 1), :]
        SB[2, 1, row] = F[2, x, pl.ds(0, 1), :]

    @pl.loop(EDGE, EDGE + ROWS)
    def _(x):
        level0(x)

    def count(condition):
        return jnp.where(condition, 1, 0)

    pl.semaphore_wait(
        barrier,
        count(has_below) + count(has_above) + count(has_left) + count(has_right)
        + jnp.minimum(chip, CHIPS) + jnp.minimum(chips - 1 - chip, CHIPS),
    )

    pieces = (pl.ds(0, 8), pl.ds(NY - 8, 8), pl.ds(8, NY - 16))

    def border(way, piece):
        here, there = (EDGE, EDGE + ROWS) if way == 0 else (ROWS, 0)
        return pltpu.make_async_remote_copy(
            src_ref=F.at[:, pl.ds(here, EDGE), pieces[piece]], dst_ref=F.at[:, pl.ds(there, EDGE), pieces[piece]],
            send_sem=x_send.at[way, piece], recv_sem=x_recv.at[way, piece],
            device_id={"gx": gx - 1} if way == 0 else {"gx": gx + 1}, device_id_type=MESH,
        )

    def each_border(which, act):
        for piece in which:
            pl.when(has_left)(functools.partial(lambda p: act(border(0, p), 0), piece))
            pl.when(has_right)(functools.partial(lambda p: act(border(1, p), 1), piece))

    def border_arrives(which):
        for piece in which:
            pl.when(has_right)(functools.partial(lambda p: border(0, p).wait_recv(), piece))
            pl.when(has_left)(functools.partial(lambda p: border(1, p).wait_recv(), piece))

    each_border((0, 1), lambda copy, _: copy.start())

    middle = pl.ds(8, 8)

    def far(m):
        where = {"gy": gy - 1} if m in LEFT_BOUND else {"gy": gy + 1}
        return pltpu.make_async_remote_copy(
            src_ref=SB.at[m, :, middle], dst_ref=RB.at[m, :, middle],
            send_sem=far_send.at[m], recv_sem=far_recv.at[m], device_id=where, device_id_type=MESH,
        )

    def sends(m):
        return has_below if m in LEFT_BOUND else has_above

    def receives(m):
        return has_above if m in LEFT_BOUND else has_below

    def post(m):
        pl.when(sends(m))(lambda: far(m).start())

    post(0)
    post(1)
    post(2)

    each_border((2,), lambda copy, _: copy.start())
    border_arrives((0, 1))

    for x in (*range(0, EDGE), *range(EDGE + ROWS, WIDE)):
        level0(x)
    def half(x):
        outside = (jnp.logical_not(has_left) & (x < EDGE)) | (jnp.logical_not(has_right) & (x >= EDGE + ROWS))
        return jnp.where(outside, 0.0, courant).astype(F32)

    def up(v):
        return jnp.where(lane < NZ - 1, pltpu.roll(v, NZ - 1, 1), 0.0)

    def down(v):
        return jnp.where(lane > 0, pltpu.roll(v, 1, 1), 0.0)

    def step_strips(step, old, new, c_of, e_ahead, h_behind):
        for x in range(step, WIDE - 1 - step):
            s = half(x)
            for side in range(2):
                ex, ey, ez = (old(side, k, x) for k in range(3))
                ahead = e_ahead(side, x)
                new[side, 3, x] = old(side, 3, x) - s * ((ahead(ez, 1) - ez) - (up(ey) - ey))
                new[side, 4, x] = old(side, 4, x) - s * ((up(ex) - ex) - (old(side, 2, x + 1) - ez))
                new[side, 5, x] = old(side, 5, x) - s * ((old(side, 1, x + 1) - ey) - (ahead(ex, 0) - ex))
        for x in range(step + 1, WIDE - 1 - step):
            for side in range(2):
                hx, hy, hz = (new[side, k, x] for k in range(3, 6))
                behind = h_behind(side, x)
                c = c_of(side, x)
                new[side, 0, x] = old(side, 0, x) + c * ((hz - behind(hz, 1)) - (hy - down(hy)))
                new[side, 1, x] = old(side, 1, x) + c * ((hx - down(hx)) - (hz - new[side, 5, x - 1]))
                new[side, 2, x] = old(side, 2, x) + c * ((hy - new[side, 4, x - 1]) - (hx - behind(hx, 0)))

    tile = (pl.ds(0, 8), pl.ds(NY - 8, 8))

    def from_block(side, k, x):
        return F[k, x, tile[side], :]

    def from_strip(side, k, x):
        return T[side, k, x]

    def closed_ahead(side, x):
        return lambda v, _: jnp.where(sub < 7, pltpu.roll(v, 7, 0), 0.0)

    def closed_behind(side, x):
        return lambda v, _: jnp.where(sub > 0, pltpu.roll(v, 1, 0), 0.0)

    for step in range(ITERS):
        step_strips(
            step, from_block if step == 0 else from_strip, T,
            lambda side, x: from_block(side, 6, x), closed_ahead, closed_behind,
        )
        for x in range(step, WIDE - 1 - step):
            row = pl.ds(x + 4, 1)
            SB[6 + step, 0, row] = T[1, 3, x, pl.ds(7, 1), :]
            SB[6 + step, 1, row] = T[1, 5, x, pl.ds(7, 1), :]
        post(6 + step)
        if step < ITERS - 1:
            for x in range(step + 1, WIDE - 1 - step):
                row = pl.ds(x + 4, 1)
                SB[3 + step, 0, row] = T[0, 0, x, pl.ds(0, 1), :]
                SB[3 + step, 1, row] = T[0, 2, x, pl.ds(0, 1), :]
            post(3 + step)

    border_arrives((2,))
    each_border((0, 1, 2), lambda copy, _: copy.wait_send())
    loads[2].wait()
    loads[3].wait()

    def next_y(v):
        return jnp.where(iy < NY - 1, pltpu.roll(v, NY - 1, 0), 0.0)

    def last_y(v):
        return jnp.where(iy > 0, pltpu.roll(v, 1, 0), 0.0)

    def next_z(v):
        return jnp.where(iz < NZ - 1, pltpu.roll(v, NZ - 1, 1), 0.0)

    def last_z(v):
        return jnp.where(iz > 0, pltpu.roll(v, 1, 1), 0.0)

    def magnetic(x):
        s = half(x)
        ex, ey, ez = F[0, x], F[1, x], F[2, x]
        return (
            F[3, x] - s * ((next_y(ez) - ez) - (next_z(ey) - ey)),
            F[4, x] - s * ((next_z(ex) - ex) - (F[2, x + 1] - ez)),
            F[5, x] - s * ((F[1, x + 1] - ey) - (next_y(ex) - ex)),
        )

    def electric(x):
        hx, hy, hz = F[3, x], F[4, x], F[5, x]
        c = F[6, x]
        return (
            F[0, x] + c * ((hz - last_y(hz)) - (hy - last_z(hy))),
            F[1, x] + c * ((hx - last_z(hx)) - (hz - F[5, x - 1])),
            F[2, x] + c * ((hy - F[4, x - 1]) - (hx - last_y(hx))),
        )

    def rows_of(first, trips, group, compute, base):
        @pl.loop(0, trips)
        def _(i):
            rows = [first + group * i + j for j in range(group)]
            values = [compute(x) for x in rows]
            for x, value in zip(rows, values):
                for k in range(3):
                    F[base + k, x] = value[k]

    G[...] = jnp.zeros(G.shape, F32)

    @pl.loop(0, ITERS)
    def _(t):
        rows_of(0, 5, 3, magnetic, 3)
        rows_of(1, 7, 2, electric, 0)

        @pl.loop(0, ROWS // 2)
        def _(i):
            for r in (2 * i, 2 * i + 1):
                x = r + EDGE
                G[r] = G[r] + (
                    FE[t, 0, r].astype(F32) * F[0, x] + FE[t, 1, r].astype(F32) * F[1, x]
                    + FE[t, 2, r].astype(F32) * F[2, x]
                )

    for k in range(6):
        for side in range(2):
            D[side, k] = jnp.zeros((WIDE, 8, NZ), F32)

    lower = sub < 4

    def gather(W, direct, z_send, z_recv, p_send, p_recv):
        def slot(s):
            return W.at[pl.ds(ROWS * s, ROWS)]

        def relay(way, k):
            sign = -1 if way == 0 else 1
            return pltpu.make_async_remote_copy(
                src_ref=slot(8 if direct else 8 + sign * 2 * (k - 1)), dst_ref=slot(8 + sign * 2 * k),
                send_sem=z_send.at[way, k - 1], recv_sem=z_recv.at[way, k - 1],
                device_id={"gx": gx - 2 * sign * (k if direct else 1)}, device_id_type=MESH,
            )

        exists = chip_at

        def relays(way, k):
            if direct:
                return chip_at(1 - way, k)
            onward = chip_at(1 - way, 1)
            return onward if k == 1 else onward & exists(way, k - 1)

        def across(way, k):
            sign = -1 if way == 0 else 1
            s = 8 + sign * 2 * k
            i = s // 2 - 1 + core
            return pltpu.make_async_remote_copy(
                src_ref=slot(s), dst_ref=slot(2 * i + 1),
                send_sem=p_send.at[s // 2], recv_sem=p_recv.at[i],
                device_id={"gx": gx + 1 - 2 * core}, device_id_type=MESH,
            )

        def crosses(way, k):
            if k == 0:
                return None
            known = exists(way, k)
            if k == CHIPS:
                known = known & (core == 1 if way == 0 else core == 0)
            return known

        def begin():
            for k in range(CHIPS if direct else 1, 0, -1):
                for way in (0, 1):
                    pl.when(relays(way, k))(functools.partial(lambda w, j: relay(w, j).start(), way, k))
            across(0, 0).start()

        def step(k):
            for way in (0, 1):
                pl.when(exists(way, k))(functools.partial(lambda w: relay(w, k).wait_recv(), way))
                if k < CHIPS and not direct:
                    pl.when(relays(way, k + 1))(functools.partial(lambda w: relay(w, k + 1).start(), way))
                pl.when(crosses(way, k))(functools.partial(lambda w: across(w, k).start(), way))

        def finish():
            for i in range(8):
                other = gx + 2 * i + 1 - 8
                copy = pltpu.make_async_remote_copy(
                    src_ref=slot(2 * i + 1), dst_ref=slot(2 * i + 1),
                    send_sem=p_send.at[0], recv_sem=p_recv.at[i],
                    device_id={"gx": gx + 1 - 2 * core}, device_id_type=MESH,
                )
                pl.when((other >= 0) & (other < nx))(copy.wait_recv)

        def drain():
            across(0, 0).wait_send()
            for k in range(1, CHIPS + 1):
                for way in (0, 1):
                    pl.when(relays(way, k))(functools.partial(lambda w, j: relay(w, j).wait_send(), way, k))
                    pl.when(crosses(way, k))(functools.partial(lambda w, j: across(w, j).wait_send(), way, k))

        return begin, step, finish, drain

    begin_a, step_a, finish_a, drain_a = gather(WA, False, za_send, za_recv, pa_send, pa_recv)
    begin_b, step_b, finish_b, drain_b = gather(WB, False, zb_send, zb_recv, pb_send, pb_recv)

    @pl.loop(0, ROWS)
    def _(r):
        m = G[r] * MV[r].astype(F32)
        WA[8 * ROWS + r, pl.ds(0, 16), :] = m[8:24]
        WA[8 * ROWS + r, pl.ds(16, 8), :] = jnp.where(lower, m[24:32], m[0:8])


    def forward(m, way):
        tile = 2 if way == 0 else 0
        where = {"gx": gx - 1} if way == 0 else {"gx": gx + 1}
        return pltpu.make_async_remote_copy(
            src_ref=RB.at[m, :, middle], dst_ref=RB.at[m, :, pl.ds(8 * tile, 8)],
            send_sem=fwd_send.at[m, way], recv_sem=fwd_recv.at[m, way], device_id=where, device_id_type=MESH,
        )

    begin_a()
    order = (0, 1, 2, 6, 3, 7, 4, 8, 5, 9)
    for m in order:
        pl.when(receives(m))(functools.partial(lambda i: far(i).wait_recv(), m))
        pl.when(receives(m) & has_left)(functools.partial(lambda i: forward(i, 0).start(), m))
        pl.when(receives(m) & has_right)(functools.partial(lambda i: forward(i, 1).start(), m))

    def arrived(m):
        pl.when(receives(m) & has_right)(functools.partial(lambda i: forward(i, 0).wait_recv(), m))
        pl.when(receives(m) & has_left)(functools.partial(lambda i: forward(i, 1).wait_recv(), m))

    for m in order:
        arrived(m)

    @pl.loop(0, WIDE)
    def _(x):
        row = pl.ds(x + 4, 1)
        c = F[6, x]
        near, next_near = RB[1, 0, row], RB[1, 1, row]
        CS[0, x] = jnp.where(lower, c[0:8], jnp.where(sub == 7, near, jnp.where(sub == 6, next_near, 0.0)))
        near, next_near = RB[0, 0, row], RB[0, 1, row]
        CS[1, x] = jnp.where(lower, jnp.where(sub == 0, near, jnp.where(sub == 1, next_near, 0.0)), c[24:32])

    inflow = jnp.where(has_below, 1.0, 0.0).astype(F32)

    def strip(side, k, x):
        return D[side, k, x]

    def open_ahead(step):
        def ahead_at(side, x):
            planes, row = (SB if side == 0 else RB), pl.ds(x + 4, 1)

            def ahead(v, comp):
                trace = planes[2 + step, comp, row]
                trace = trace * inflow if side == 0 else trace
                return pltpu.roll(v, 7, 0) + jnp.where(sub == 7, trace, 0.0)

            return ahead

        return ahead_at

    def open_behind(step):
        def behind_at(side, x):
            planes, row = (RB if side == 0 else SB), pl.ds(x + 4, 1)
            return lambda v, comp: pltpu.roll(v, 1, 0) + jnp.where(sub == 0, planes[6 + step, comp, row], 0.0)

        return behind_at

    half_tile = (pl.ds(0, 16), pl.ds(NY - 16, 16))
    for step in range(ITERS):
        step_strips(step, strip, D, lambda side, x: CS[side, x], open_ahead(step), open_behind(step))
        for r in range(ROWS):
            for side in range(2):
                stored = [FE[step, k, r, half_tile[side], :].astype(F32) for k in range(3)]
                stored = [v[0:8] if side == 0 else v[8:16] for v in stored]
                e = [D[side, k, r + EDGE] for k in range(3)]
                g = stored[0] * e[0] + stored[1] * e[1] + stored[2] * e[2]
                GS[side, r] = g if step == 0 else GS[side, r] + g

    @pl.loop(0, ROWS)
    def _(r):
        g = jnp.where(lower, G[r, pl.ds(0, 8), :] + GS[0, r], G[r, pl.ds(24, 8), :] + GS[1, r])
        mask = jnp.where(lower, MV[r, pl.ds(0, 8), :], MV[r, pl.ds(24, 8), :])
        WB[8 * ROWS + r] = g * mask.astype(F32)

    step_a(1)
    begin_b()

    @pl.loop(0, ROWS)
    def _(r):
        x = r + EDGE
        for k in range(3):
            e = F[k, x]
            final_ref[k, r, pl.ds(8, 16), :] = e[8:24]
            final_ref[k, r, pl.ds(0, 8), :] = e[0:8] + jnp.where(lower, D[0, k, x], 0.0)
            final_ref[k, r, pl.ds(24, 8), :] = e[24:32] + jnp.where(lower, 0.0, D[1, k, x])

    for k in range(1, CHIPS + 1):
        if k > 1:
            step_a(k)
        step_b(k)
    finish_a()
    finish_b()

    taps = [tap_ref[b] for b in range(BAND)]
    starts = [off_ref[b] + REACH for b in range(BAND)]

    @pl.loop(0, ROWS)
    def _(r):
        wide, thin = taps[0] * WA[starts[0] + r], taps[0] * WB[starts[0] + r]
        for b in range(1, BAND):
            wide = wide + taps[b] * WA[starts[b] + r]
            thin = thin + taps[b] * WB[starts[b] + r]
        mixed = wide[16:24]
        filt_ref[r, pl.ds(8, 16), :] = wide[0:16]
        filt_ref[r, pl.ds(0, 8), :] = jnp.where(lower, thin, mixed)
        filt_ref[r, pl.ds(24, 8), :] = jnp.where(lower, mixed, thin)

    for m in range(MESSAGES):
        pl.when(sends(m))(functools.partial(lambda i: far(i).wait_send(), m))
        pl.when(receives(m) & has_left)(functools.partial(lambda i: forward(i, 0).wait_send(), m))
        pl.when(receives(m) & has_right)(functools.partial(lambda i: forward(i, 1).wait_send(), m))
    drain_a()
    drain_b()


def solution(mesh):
    nx, ny = mesh.shape["gx"], mesh.shape["gy"]

    def shards(adjoint_fields, forward_e, permittivity, design_mask, band_offsets, filter_taps):
        dma = pltpu.SemaphoreType.DMA
        hbm, vmem, smem = (pl.BlockSpec(memory_space=s) for s in (pltpu.HBM, pltpu.VMEM, pltpu.SMEM))
        return pl.pallas_call(
            functools.partial(kernel, nx, ny),
            out_shape=(
                jax.ShapeDtypeStruct((ROWS, NY, NZ), F32),
                jax.ShapeDtypeStruct((3, ROWS, NY, NZ), F32),
            ),
            in_specs=[hbm, hbm, hbm, hbm, smem, smem],
            out_specs=(vmem, vmem),
            scratch_shapes=[
                pltpu.VMEM((7, WIDE, NY, NZ), F32),
                pltpu.VMEM((ITERS, 3, ROWS, NY, NZ), jnp.bfloat16),
                pltpu.VMEM((ROWS, NY, NZ), F32),
                pltpu.VMEM((ROWS, NY, NZ), jnp.int32),
                pltpu.VMEM((ROWS, NY, NZ), F32),
                pltpu.VMEM((MESSAGES, 2, 24, NZ), F32),
                pltpu.VMEM((MESSAGES, 2, 24, NZ), F32),
                pltpu.VMEM((2, 6, WIDE, 8, NZ), F32),
                pltpu.VMEM((2, 6, WIDE, 8, NZ), F32),
                pltpu.VMEM((2, WIDE, 8, NZ), F32),
                pltpu.VMEM((2, ROWS, 8, NZ), F32),
                pltpu.VMEM((17 * ROWS, 24, NZ), F32),
                pltpu.VMEM((17 * ROWS, 8, NZ), F32),
                dma((4,)), dma((2, 3)), dma((2, 3)),
                dma((MESSAGES,)), dma((MESSAGES,)), dma((MESSAGES, 2)), dma((MESSAGES, 2)),
                dma((2, CHIPS)), dma((2, CHIPS)), dma((9,)), dma((8,)),
                dma((2, CHIPS)), dma((2, CHIPS)), dma((9,)), dma((8,)),
            ],
            compiler_params=pltpu.CompilerParams(collective_id=0, has_side_effects=True, vmem_limit_bytes=16 << 20),
            name="adjoint_yee_filter",
        )(
            *(pltpu.with_memory_space_constraint(a, pltpu.HBM) for a in (adjoint_fields, forward_e, permittivity, design_mask)),
            band_offsets, filter_taps,
        )

    return jax.shard_map(
        shards,
        mesh=mesh,
        in_specs=(
            P(None, "gx", "gy", None),
            P(None, None, "gx", "gy", None),
            P("gx", "gy", None),
            P("gx", "gy", None),
            P(),
            P(),
        ),
        out_specs=(P("gx", "gy", None), P(None, "gx", "gy", None)),
        check_vma=False,
    )
```

```python
import functools

import jax
import jax.numpy as jnp
from jax import lax
from jax.experimental import pallas as pl
from jax.experimental.pallas import tpu as pltpu
from jax.sharding import PartitionSpec as P

ITERS = 4
BAND = 9
REACH = 64
courant = 0.5

MESH = pl.DeviceIdType.MESH
F32 = jnp.float32
ROWS = 8
EDGE = 4
WIDE = ROWS + 2 * EDGE
NY = 32
NZ = 128
LEFT_BOUND = (0, 2, 3, 4, 5)
RIGHT_BOUND = (1, 6, 7, 8, 9)
MESSAGES = 10
CHIPS = 4


def kernel(
    nx, ny,
    fields_hbm, stored_hbm, perm_hbm, mask_hbm, off_hbm, tap_hbm,
    filt_ref, final_ref,
    F, FE, PV, MV, G, SB, RB, T, D, CS, GS, WA, WB, off_ref, tap_ref,
    load_sem, x_send, x_recv, far_send, far_recv, fwd_send, fwd_recv,
    za_send, za_recv, pa_send, pa_recv, zb_send, zb_recv, pb_send, pb_recv,
):
    gx, gy = lax.axis_index("gx"), lax.axis_index("gy")
    core, chip, chips = gx % 2, gx // 2, nx // 2
    has_left, has_right = gx > 0, gx < nx - 1
    has_below, has_above = gy > 0, gy < ny - 1

    loads = [
        pltpu.make_async_copy(fields_hbm, F.at[pl.ds(0, 6), pl.ds(EDGE, ROWS)], load_sem.at[0]),
        pltpu.make_async_copy(perm_hbm, PV, load_sem.at[1]),
        pltpu.make_async_copy(stored_hbm, FE, load_sem.at[2]),
        pltpu.make_async_copy(mask_hbm, MV, load_sem.at[3]),
        pltpu.make_async_copy(off_hbm, off_ref, load_sem.at[4]),
        pltpu.make_async_copy(tap_hbm, tap_ref, load_sem.at[5]),
    ]
    for load in loads:
        load.start()

    def clear(ref, length):
        @pl.loop(0, length)
        def _(i):
            ref[i] = jnp.zeros(ref.shape[1:], F32)

    RB[...] = jnp.zeros(RB.shape, F32)

    @pl.when(jnp.logical_not(has_left))
    def _():
        for k in range(7):
            for r in range(EDGE):
                F[k, r] = jnp.zeros((NY, NZ), F32)

    @pl.when(jnp.logical_not(has_right))
    def _():
        for k in range(7):
            for r in range(EDGE):
                F[k, EDGE + ROWS + r] = jnp.zeros((NY, NZ), F32)

    @pl.when((gx < ROWS) | (gx >= nx - ROWS))
    def _():
        clear(WA, 17 * ROWS)
        clear(WB, 17 * ROWS)

    barrier = pltpu.get_barrier_semaphore()

    def greet(condition, where):
        @pl.when(condition)
        def _():
            pl.semaphore_signal(barrier, inc=1, device_id=where, device_id_type=MESH)

    def chip_at(way, k):
        return chip >= k if way == 0 else chip + k <= chips - 1

    up_chip, down_chip = chip_at(1, 1), chip_at(0, 1)
    greet(has_below, {"gy": gy - 1})
    greet(has_above, {"gy": gy + 1})
    greet(has_left, {"gx": gx - 1})
    greet(has_right, {"gx": gx + 1})
    for k in range(1, CHIPS + 1):
        greet(chip_at(0, k), {"gx": gx - 2 * k})
        greet(chip_at(1, k), {"gx": gx + 2 * k})

    iy = lax.broadcasted_iota(jnp.int32, (NY, NZ), 0)
    iz = lax.broadcasted_iota(jnp.int32, (NY, NZ), 1)
    sub = lax.broadcasted_iota(jnp.int32, (8, NZ), 0)
    lane = lax.broadcasted_iota(jnp.int32, (8, NZ), 1)

    loads[0].wait()
    loads[1].wait()

    @pl.loop(0, ROWS)
    def _(r):
        c = courant / PV[r]
        F[6, EDGE + r] = c
        row = pl.ds(r + 8, 1)
        SB[0, 0, row] = c[0:1]
        SB[0, 1, row] = c[1:2]
        SB[1, 0, row] = c[31:32]
        SB[1, 1, row] = c[30:31]

    def level0(x):
        row = pl.ds(x + 4, 1)
        SB[2, 0, row] = F[0, x, pl.ds(0, 1), :]
        SB[2, 1, row] = F[2, x, pl.ds(0, 1), :]

    @pl.loop(EDGE, EDGE + ROWS)
    def _(x):
        level0(x)

    def count(condition):
        return jnp.where(condition, 1, 0)

    pl.semaphore_wait(
        barrier,
        count(has_below) + count(has_above) + count(has_left) + count(has_right)
        + jnp.minimum(chip, CHIPS) + jnp.minimum(chips - 1 - chip, CHIPS),
    )

    pieces = (pl.ds(0, 8), pl.ds(NY - 8, 8), pl.ds(8, NY - 16))

    def border(way, piece):
        here, there = (EDGE, EDGE + ROWS) if way == 0 else (ROWS, 0)
        return pltpu.make_async_remote_copy(
            src_ref=F.at[:, pl.ds(here, EDGE), pieces[piece]], dst_ref=F.at[:, pl.ds(there, EDGE), pieces[piece]],
            send_sem=x_send.at[way, piece], recv_sem=x_recv.at[way, piece],
            device_id={"gx": gx - 1} if way == 0 else {"gx": gx + 1}, device_id_type=MESH,
        )

    def each_border(which, act):
        for piece in which:
            pl.when(has_left)(functools.partial(lambda p: act(border(0, p), 0), piece))
            pl.when(has_right)(functools.partial(lambda p: act(border(1, p), 1), piece))

    def border_arrives(which):
        for piece in which:
            pl.when(has_right)(functools.partial(lambda p: border(0, p).wait_recv(), piece))
            pl.when(has_left)(functools.partial(lambda p: border(1, p).wait_recv(), piece))

    each_border((0, 1), lambda copy, _: copy.start())

    middle = pl.ds(8, 8)

    def far(m):
        where = {"gy": gy - 1} if m in LEFT_BOUND else {"gy": gy + 1}
        return pltpu.make_async_remote_copy(
            src_ref=SB.at[m, :, middle], dst_ref=RB.at[m, :, middle],
            send_sem=far_send.at[m], recv_sem=far_recv.at[m], device_id=where, device_id_type=MESH,
        )

    def sends(m):
        return has_below if m in LEFT_BOUND else has_above

    def receives(m):
        return has_above if m in LEFT_BOUND else has_below

    def post(m):
        pl.when(sends(m))(lambda: far(m).start())

    post(0)
    post(1)
    post(2)

    each_border((2,), lambda copy, _: copy.start())
    border_arrives((0, 1))

    for x in (*range(0, EDGE), *range(EDGE + ROWS, WIDE)):
        level0(x)
    def half(x):
        outside = (jnp.logical_not(has_left) & (x < EDGE)) | (jnp.logical_not(has_right) & (x >= EDGE + ROWS))
        return jnp.where(outside, 0.0, courant).astype(F32)

    def up(v):
        return jnp.where(lane < NZ - 1, pltpu.roll(v, NZ - 1, 1), 0.0)

    def down(v):
        return jnp.where(lane > 0, pltpu.roll(v, 1, 1), 0.0)

    def step_strips(step, old, new, c_of, e_ahead, h_behind):
        for x in range(step, WIDE - 1 - step):
            s = half(x)
            for side in range(2):
                ex, ey, ez = (old(side, k, x) for k in range(3))
                ahead = e_ahead(side, x)
                new[side, 3, x] = old(side, 3, x) - s * ((ahead(ez, 1) - ez) - (up(ey) - ey))
                new[side, 4, x] = old(side, 4, x) - s * ((up(ex) - ex) - (old(side, 2, x + 1) - ez))
                new[side, 5, x] = old(side, 5, x) - s * ((old(side, 1, x + 1) - ey) - (ahead(ex, 0) - ex))
        for x in range(step + 1, WIDE - 1 - step):
            for side in range(2):
                hx, hy, hz = (new[side, k, x] for k in range(3, 6))
                behind = h_behind(side, x)
                c = c_of(side, x)
                new[side, 0, x] = old(side, 0, x) + c * ((hz - behind(hz, 1)) - (hy - down(hy)))
                new[side, 1, x] = old(side, 1, x) + c * ((hx - down(hx)) - (hz - new[side, 5, x - 1]))
                new[side, 2, x] = old(side, 2, x) + c * ((hy - new[side, 4, x - 1]) - (hx - behind(hx, 0)))

    tile = (pl.ds(0, 8), pl.ds(NY - 8, 8))

    def from_block(side, k, x):
        return F[k, x, tile[side], :]

    def from_strip(side, k, x):
        return T[side, k, x]

    def closed_ahead(side, x):
        return lambda v, _: jnp.where(sub < 7, pltpu.roll(v, 7, 0), 0.0)

    def closed_behind(side, x):
        return lambda v, _: jnp.where(sub > 0, pltpu.roll(v, 1, 0), 0.0)

    for step in range(ITERS):
        step_strips(
            step, from_block if step == 0 else from_strip, T,
            lambda side, x: from_block(side, 6, x), closed_ahead, closed_behind,
        )
        for x in range(step, WIDE - 1 - step):
            row = pl.ds(x + 4, 1)
            SB[6 + step, 0, row] = T[1, 3, x, pl.ds(7, 1), :]
            SB[6 + step, 1, row] = T[1, 5, x, pl.ds(7, 1), :]
        post(6 + step)
        if step < ITERS - 1:
            for x in range(step + 1, WIDE - 1 - step):
                row = pl.ds(x + 4, 1)
                SB[3 + step, 0, row] = T[0, 0, x, pl.ds(0, 1), :]
                SB[3 + step, 1, row] = T[0, 2, x, pl.ds(0, 1), :]
            post(3 + step)

    border_arrives((2,))
    each_border((0, 1, 2), lambda copy, _: copy.wait_send())
    loads[2].wait()
    for load in loads[3:]:
        load.wait()

    def next_y(v):
        return jnp.where(iy < NY - 1, pltpu.roll(v, NY - 1, 0), 0.0)

    def last_y(v):
        return jnp.where(iy > 0, pltpu.roll(v, 1, 0), 0.0)

    def next_z(v):
        return jnp.where(iz < NZ - 1, pltpu.roll(v, NZ - 1, 1), 0.0)

    def last_z(v):
        return jnp.where(iz > 0, pltpu.roll(v, 1, 1), 0.0)

    def magnetic(x):
        s = half(x)
        ex, ey, ez = F[0, x], F[1, x], F[2, x]
        return (
            F[3, x] - s * ((next_y(ez) - ez) - (next_z(ey) - ey)),
            F[4, x] - s * ((next_z(ex) - ex) - (F[2, x + 1] - ez)),
            F[5, x] - s * ((F[1, x + 1] - ey) - (next_y(ex) - ex)),
        )

    def electric(x):
        hx, hy, hz = F[3, x], F[4, x], F[5, x]
        c = F[6, x]
        return (
            F[0, x] + c * ((hz - last_y(hz)) - (hy - last_z(hy))),
            F[1, x] + c * ((hx - last_z(hx)) - (hz - F[5, x - 1])),
            F[2, x] + c * ((hy - F[4, x - 1]) - (hx - last_y(hx))),
        )

    def rows_of(first, trips, group, compute, base):
        @pl.loop(0, trips)
        def _(i):
            rows = [first + group * i + j for j in range(group)]
            values = [compute(x) for x in rows]
            for x, value in zip(rows, values):
                for k in range(3):
                    F[base + k, x] = value[k]

    G[...] = jnp.zeros(G.shape, F32)

    @pl.loop(0, ITERS)
    def _(t):
        rows_of(0, 5, 3, magnetic, 3)
        rows_of(1, 7, 2, electric, 0)

        @pl.loop(0, ROWS // 2)
        def _(i):
            for r in (2 * i, 2 * i + 1):
                x = r + EDGE
                G[r] = G[r] + (
                    FE[t, 0, r].astype(F32) * F[0, x] + FE[t, 1, r].astype(F32) * F[1, x]
                    + FE[t, 2, r].astype(F32) * F[2, x]
                )

    for k in range(6):
        for side in range(2):
            D[side, k] = jnp.zeros((WIDE, 8, NZ), F32)

    lower = sub < 4

    def gather(W, direct, z_send, z_recv, p_send, p_recv):
        def slot(s):
            return W.at[pl.ds(ROWS * s, ROWS)]

        def relay(way, k):
            sign = -1 if way == 0 else 1
            return pltpu.make_async_remote_copy(
                src_ref=slot(8 if direct else 8 + sign * 2 * (k - 1)), dst_ref=slot(8 + sign * 2 * k),
                send_sem=z_send.at[way, k - 1], recv_sem=z_recv.at[way, k - 1],
                device_id={"gx": gx - 2 * sign * (k if direct else 1)}, device_id_type=MESH,
            )

        exists = chip_at

        def relays(way, k):
            if direct:
                return chip_at(1 - way, k)
            onward = chip_at(1 - way, 1)
            return onward if k == 1 else onward & exists(way, k - 1)

        def across(way, k):
            sign = -1 if way == 0 else 1
            s = 8 + sign * 2 * k
            i = s // 2 - 1 + core
            return pltpu.make_async_remote_copy(
                src_ref=slot(s), dst_ref=slot(2 * i + 1),
                send_sem=p_send.at[s // 2], recv_sem=p_recv.at[i],
                device_id={"gx": gx + 1 - 2 * core}, device_id_type=MESH,
            )

        def crosses(way, k):
            if k == 0:
                return None
            known = exists(way, k)
            if k == CHIPS:
                known = known & (core == 1 if way == 0 else core == 0)
            return known

        def begin():
            for k in range(CHIPS if direct else 1, 0, -1):
                for way in (0, 1):
                    pl.when(relays(way, k))(functools.partial(lambda w, j: relay(w, j).start(), way, k))
            across(0, 0).start()

        def step(k):
            for way in (0, 1):
                pl.when(exists(way, k))(functools.partial(lambda w: relay(w, k).wait_recv(), way))
                if k < CHIPS and not direct:
                    pl.when(relays(way, k + 1))(functools.partial(lambda w: relay(w, k + 1).start(), way))
                pl.when(crosses(way, k))(functools.partial(lambda w: across(w, k).start(), way))

        def finish():
            for i in range(8):
                other = gx + 2 * i + 1 - 8
                copy = pltpu.make_async_remote_copy(
                    src_ref=slot(2 * i + 1), dst_ref=slot(2 * i + 1),
                    send_sem=p_send.at[0], recv_sem=p_recv.at[i],
                    device_id={"gx": gx + 1 - 2 * core}, device_id_type=MESH,
                )
                pl.when((other >= 0) & (other < nx))(copy.wait_recv)

        def drain():
            across(0, 0).wait_send()
            for k in range(1, CHIPS + 1):
                for way in (0, 1):
                    pl.when(relays(way, k))(functools.partial(lambda w, j: relay(w, j).wait_send(), way, k))
                    pl.when(crosses(way, k))(functools.partial(lambda w, j: across(w, j).wait_send(), way, k))

        return begin, step, finish, drain

    begin_a, step_a, finish_a, drain_a = gather(WA, False, za_send, za_recv, pa_send, pa_recv)
    begin_b, step_b, finish_b, drain_b = gather(WB, False, zb_send, zb_recv, pb_send, pb_recv)

    @pl.loop(0, ROWS)
    def _(r):
        m = G[r] * MV[r].astype(F32)
        WA[8 * ROWS + r, pl.ds(0, 16), :] = m[8:24]
        WA[8 * ROWS + r, pl.ds(16, 8), :] = jnp.where(lower, m[24:32], m[0:8])


    def forward(m, way):
        tile = 2 if way == 0 else 0
        where = {"gx": gx - 1} if way == 0 else {"gx": gx + 1}
        return pltpu.make_async_remote_copy(
            src_ref=RB.at[m, :, middle], dst_ref=RB.at[m, :, pl.ds(8 * tile, 8)],
            send_sem=fwd_send.at[m, way], recv_sem=fwd_recv.at[m, way], device_id=where, device_id_type=MESH,
        )

    begin_a()
    order = (0, 1, 2, 6, 3, 7, 4, 8, 5, 9)
    for m in order:
        pl.when(receives(m))(functools.partial(lambda i: far(i).wait_recv(), m))
        pl.when(receives(m) & has_left)(functools.partial(lambda i: forward(i, 0).start(), m))
        pl.when(receives(m) & has_right)(functools.partial(lambda i: forward(i, 1).start(), m))

    def arrived(m):
        pl.when(receives(m) & has_right)(functools.partial(lambda i: forward(i, 0).wait_recv(), m))
        pl.when(receives(m) & has_left)(functools.partial(lambda i: forward(i, 1).wait_recv(), m))

    for m in order:
        arrived(m)

    @pl.loop(0, WIDE)
    def _(x):
        row = pl.ds(x + 4, 1)
        c = F[6, x]
        near, next_near = RB[1, 0, row], RB[1, 1, row]
        CS[0, x] = jnp.where(lower, c[0:8], jnp.where(sub == 7, near, jnp.where(sub == 6, next_near, 0.0)))
        near, next_near = RB[0, 0, row], RB[0, 1, row]
        CS[1, x] = jnp.where(lower, jnp.where(sub == 0, near, jnp.where(sub == 1, next_near, 0.0)), c[24:32])

    inflow = jnp.where(has_below, 1.0, 0.0).astype(F32)

    def strip(side, k, x):
        return D[side, k, x]

    def open_ahead(step):
        def ahead_at(side, x):
            planes, row = (SB if side == 0 else RB), pl.ds(x + 4, 1)

            def ahead(v, comp):
                trace = planes[2 + step, comp, row]
                trace = trace * inflow if side == 0 else trace
                return pltpu.roll(v, 7, 0) + jnp.where(sub == 7, trace, 0.0)

            return ahead

        return ahead_at

    def open_behind(step):
        def behind_at(side, x):
            planes, row = (RB if side == 0 else SB), pl.ds(x + 4, 1)
            return lambda v, comp: pltpu.roll(v, 1, 0) + jnp.where(sub == 0, planes[6 + step, comp, row], 0.0)

        return behind_at

    half_tile = (pl.ds(0, 16), pl.ds(NY - 16, 16))
    for step in range(ITERS):
        step_strips(step, strip, D, lambda side, x: CS[side, x], open_ahead(step), open_behind(step))
        for r in range(ROWS):
            for side in range(2):
                stored = [FE[step, k, r, half_tile[side], :].astype(F32) for k in range(3)]
                stored = [v[0:8] if side == 0 else v[8:16] for v in stored]
                e = [D[side, k, r + EDGE] for k in range(3)]
                g = stored[0] * e[0] + stored[1] * e[1] + stored[2] * e[2]
                GS[side, r] = g if step == 0 else GS[side, r] + g

    @pl.loop(0, ROWS)
    def _(r):
        g = jnp.where(lower, G[r, pl.ds(0, 8), :] + GS[0, r], G[r, pl.ds(24, 8), :] + GS[1, r])
        mask = jnp.where(lower, MV[r, pl.ds(0, 8), :], MV[r, pl.ds(24, 8), :])
        WB[8 * ROWS + r] = g * mask.astype(F32)

    step_a(1)
    begin_b()

    @pl.loop(0, ROWS)
    def _(r):
        x = r + EDGE
        for k in range(3):
            e = F[k, x]
            final_ref[k, r, pl.ds(8, 16), :] = e[8:24]
            final_ref[k, r, pl.ds(0, 8), :] = e[0:8] + jnp.where(lower, D[0, k, x], 0.0)
            final_ref[k, r, pl.ds(24, 8), :] = e[24:32] + jnp.where(lower, 0.0, D[1, k, x])

    for k in range(1, CHIPS + 1):
        if k > 1:
            step_a(k)
        step_b(k)
    finish_a()
    finish_b()

    taps = [tap_ref[b] for b in range(BAND)]
    starts = [off_ref[b] + REACH for b in range(BAND)]

    @pl.loop(0, ROWS)
    def _(r):
        wide, thin = taps[0] * WA[starts[0] + r], taps[0] * WB[starts[0] + r]
        for b in range(1, BAND):
            wide = wide + taps[b] * WA[starts[b] + r]
            thin = thin + taps[b] * WB[starts[b] + r]
        mixed = wide[16:24]
        filt_ref[r, pl.ds(8, 16), :] = wide[0:16]
        filt_ref[r, pl.ds(0, 8), :] = jnp.where(lower, thin, mixed)
        filt_ref[r, pl.ds(24, 8), :] = jnp.where(lower, mixed, thin)

    for m in range(MESSAGES):
        pl.when(sends(m))(functools.partial(lambda i: far(i).wait_send(), m))
        pl.when(receives(m) & has_left)(functools.partial(lambda i: forward(i, 0).wait_send(), m))
        pl.when(receives(m) & has_right)(functools.partial(lambda i: forward(i, 1).wait_send(), m))
    drain_a()
    drain_b()


def solution(mesh):
    nx, ny = mesh.shape["gx"], mesh.shape["gy"]

    def shards(*arguments):
        dma = pltpu.SemaphoreType.DMA
        hbm, vmem = (pl.BlockSpec(memory_space=s) for s in (pltpu.HBM, pltpu.VMEM))
        return pl.pallas_call(
            functools.partial(kernel, nx, ny),
            out_shape=(
                jax.ShapeDtypeStruct((ROWS, NY, NZ), F32),
                jax.ShapeDtypeStruct((3, ROWS, NY, NZ), F32),
            ),
            in_specs=[hbm] * 6,
            out_specs=(vmem, vmem),
            scratch_shapes=[
                pltpu.VMEM((7, WIDE, NY, NZ), F32),
                pltpu.VMEM((ITERS, 3, ROWS, NY, NZ), jnp.bfloat16),
                pltpu.VMEM((ROWS, NY, NZ), F32),
                pltpu.VMEM((ROWS, NY, NZ), jnp.int32),
                pltpu.VMEM((ROWS, NY, NZ), F32),
                pltpu.VMEM((MESSAGES, 2, 24, NZ), F32),
                pltpu.VMEM((MESSAGES, 2, 24, NZ), F32),
                pltpu.VMEM((2, 6, WIDE, 8, NZ), F32),
                pltpu.VMEM((2, 6, WIDE, 8, NZ), F32),
                pltpu.VMEM((2, WIDE, 8, NZ), F32),
                pltpu.VMEM((2, ROWS, 8, NZ), F32),
                pltpu.VMEM((17 * ROWS, 24, NZ), F32),
                pltpu.VMEM((17 * ROWS, 8, NZ), F32),
                pltpu.SMEM((BAND,), jnp.int32), pltpu.SMEM((BAND,), F32),
                dma((6,)), dma((2, 3)), dma((2, 3)),
                dma((MESSAGES,)), dma((MESSAGES,)), dma((MESSAGES, 2)), dma((MESSAGES, 2)),
                dma((2, CHIPS)), dma((2, CHIPS)), dma((9,)), dma((8,)),
                dma((2, CHIPS)), dma((2, CHIPS)), dma((9,)), dma((8,)),
            ],
            compiler_params=pltpu.CompilerParams(collective_id=0, has_side_effects=True, vmem_limit_bytes=16 << 20),
            name="adjoint_yee_filter",
        )(
            *(pltpu.with_memory_space_constraint(a, pltpu.HBM) for a in arguments),
        )

    return jax.shard_map(
        shards,
        mesh=mesh,
        in_specs=(
            P(None, "gx", "gy", None),
            P(None, None, "gx", "gy", None),
            P("gx", "gy", None),
            P("gx", "gy", None),
            P(),
            P(),
        ),
        out_specs=(P("gx", "gy", None), P(None, "gx", "gy", None)),
        check_vma=False,
    )
```

```python
import functools

import jax
import jax.numpy as jnp
from jax import lax
from jax.experimental import pallas as pl
from jax.experimental.pallas import tpu as pltpu
from jax.sharding import PartitionSpec as P

ITERS = 4
BAND = 9
REACH = 64
courant = 0.5

MESH = pl.DeviceIdType.MESH
F32 = jnp.float32
ROWS = 8
EDGE = 4
WIDE = ROWS + 2 * EDGE
NY = 32
NZ = 128
LEFT_BOUND = (0, 2, 3, 4, 5)
RIGHT_BOUND = (1, 6, 7, 8, 9)
MESSAGES = 10
CHIPS = 4


def kernel(
    nx, ny,
    fields_hbm, stored_hbm, perm_hbm, mask_hbm, off_hbm, tap_hbm,
    filt_ref, final_ref,
    F, FE, PV, MV, G, SB, RB, T, D, CS, GS, WA, WB, off_ref, tap_ref,
    load_sem, x_send, x_recv, far_send, far_recv, fwd_send, fwd_recv,
    za_send, za_recv, pa_send, pa_recv, zb_send, zb_recv, pb_send, pb_recv,
):
    gx, gy = lax.axis_index("gx"), lax.axis_index("gy")
    core, chip, chips = gx % 2, gx // 2, nx // 2
    has_left, has_right = gx > 0, gx < nx - 1
    has_below, has_above = gy > 0, gy < ny - 1

    loads = [
        pltpu.make_async_copy(fields_hbm, F.at[pl.ds(0, 6), pl.ds(EDGE, ROWS)], load_sem.at[0]),
        pltpu.make_async_copy(perm_hbm, PV, load_sem.at[1]),
        pltpu.make_async_copy(stored_hbm, FE, load_sem.at[2]),
        pltpu.make_async_copy(mask_hbm, MV, load_sem.at[3]),
        pltpu.make_async_copy(off_hbm, off_ref, load_sem.at[4]),
        pltpu.make_async_copy(tap_hbm, tap_ref, load_sem.at[5]),
    ]
    for load in loads:
        load.start()

    def clear(ref, length):
        @pl.loop(0, length)
        def _(i):
            ref[i] = jnp.zeros(ref.shape[1:], F32)

    RB[...] = jnp.zeros(RB.shape, F32)

    @pl.when(jnp.logical_not(has_left))
    def _():
        for k in range(7):
            for r in range(EDGE):
                F[k, r] = jnp.zeros((NY, NZ), F32)

    @pl.when(jnp.logical_not(has_right))
    def _():
        for k in range(7):
            for r in range(EDGE):
                F[k, EDGE + ROWS + r] = jnp.zeros((NY, NZ), F32)

    @pl.when((gx < ROWS) | (gx >= nx - ROWS))
    def _():
        clear(WA, 17 * ROWS)
        clear(WB, 17 * ROWS)

    barrier = pltpu.get_barrier_semaphore()

    def greet(condition, where):
        @pl.when(condition)
        def _():
            pl.semaphore_signal(barrier, inc=1, device_id=where, device_id_type=MESH)

    def chip_at(way, k):
        return chip >= k if way == 0 else chip + k <= chips - 1

    up_chip, down_chip = chip_at(1, 1), chip_at(0, 1)
    greet(has_below, {"gy": gy - 1})
    greet(has_above, {"gy": gy + 1})
    greet(has_left, {"gx": gx - 1})
    greet(has_right, {"gx": gx + 1})
    greet(down_chip, {"gx": gx - 2})
    greet(up_chip, {"gx": gx + 2})

    iy = lax.broadcasted_iota(jnp.int32, (NY, NZ), 0)
    iz = lax.broadcasted_iota(jnp.int32, (NY, NZ), 1)
    sub = lax.broadcasted_iota(jnp.int32, (8, NZ), 0)
    lane = lax.broadcasted_iota(jnp.int32, (8, NZ), 1)

    loads[0].wait()
    loads[1].wait()

    @pl.loop(0, ROWS)
    def _(r):
        c = courant / PV[r]
        F[6, EDGE + r] = c
        row = pl.ds(r + 8, 1)
        SB[0, 0, row] = c[0:1]
        SB[0, 1, row] = c[1:2]
        SB[1, 0, row] = c[31:32]
        SB[1, 1, row] = c[30:31]

    def level0(x):
        row = pl.ds(x + 4, 1)
        SB[2, 0, row] = F[0, x, pl.ds(0, 1), :]
        SB[2, 1, row] = F[2, x, pl.ds(0, 1), :]

    @pl.loop(EDGE, EDGE + ROWS)
    def _(x):
        level0(x)

    def count(condition):
        return jnp.where(condition, 1, 0)

    pl.semaphore_wait(
        barrier,
        count(has_below) + count(has_above) + count(has_left) + count(has_right)
        + count(down_chip) + count(up_chip),
    )

    pieces = (pl.ds(0, 8), pl.ds(NY - 8, 8), pl.ds(8, NY - 16))

    def border(way, piece):
        here, there = (EDGE, EDGE + ROWS) if way == 0 else (ROWS, 0)
        return pltpu.make_async_remote_copy(
            src_ref=F.at[:, pl.ds(here, EDGE), pieces[piece]], dst_ref=F.at[:, pl.ds(there, EDGE), pieces[piece]],
            send_sem=x_send.at[way, piece], recv_sem=x_recv.at[way, piece],
            device_id={"gx": gx - 1} if way == 0 else {"gx": gx + 1}, device_id_type=MESH,
        )

    def each_border(which, act):
        for piece in which:
            pl.when(has_left)(functools.partial(lambda p: act(border(0, p), 0), piece))
            pl.when(has_right)(functools.partial(lambda p: act(border(1, p), 1), piece))

    def border_arrives(which):
        for piece in which:
            pl.when(has_right)(functools.partial(lambda p: border(0, p).wait_recv(), piece))
            pl.when(has_left)(functools.partial(lambda p: border(1, p).wait_recv(), piece))

    each_border((0, 1), lambda copy, _: copy.start())

    middle = pl.ds(8, 8)

    def far(m):
        where = {"gy": gy - 1} if m in LEFT_BOUND else {"gy": gy + 1}
        return pltpu.make_async_remote_copy(
            src_ref=SB.at[m, :, middle], dst_ref=RB.at[m, :, middle],
            send_sem=far_send.at[m], recv_sem=far_recv.at[m], device_id=where, device_id_type=MESH,
        )

    def sends(m):
        return has_below if m in LEFT_BOUND else has_above

    def receives(m):
        return has_above if m in LEFT_BOUND else has_below

    def post(m):
        pl.when(sends(m))(lambda: far(m).start())

    post(0)
    post(1)
    post(2)

    each_border((2,), lambda copy, _: copy.start())
    border_arrives((0, 1))

    for x in (*range(0, EDGE), *range(EDGE + ROWS, WIDE)):
        level0(x)
    def half(x):
        outside = (jnp.logical_not(has_left) & (x < EDGE)) | (jnp.logical_not(has_right) & (x >= EDGE + ROWS))
        return jnp.where(outside, 0.0, courant).astype(F32)

    def up(v):
        return jnp.where(lane < NZ - 1, pltpu.roll(v, NZ - 1, 1), 0.0)

    def down(v):
        return jnp.where(lane > 0, pltpu.roll(v, 1, 1), 0.0)

    def step_strips(step, old, new, c_of, e_ahead, h_behind):
        for x in range(step, WIDE - 1 - step):
            s = half(x)
            for side in range(2):
                ex, ey, ez = (old(side, k, x) for k in range(3))
                ahead = e_ahead(side, x)
                new[side, 3, x] = old(side, 3, x) - s * ((ahead(ez, 1) - ez) - (up(ey) - ey))
                new[side, 4, x] = old(side, 4, x) - s * ((up(ex) - ex) - (old(side, 2, x + 1) - ez))
                new[side, 5, x] = old(side, 5, x) - s * ((old(side, 1, x + 1) - ey) - (ahead(ex, 0) - ex))
        for x in range(step + 1, WIDE - 1 - step):
            for side in range(2):
                hx, hy, hz = (new[side, k, x] for k in range(3, 6))
                behind = h_behind(side, x)
                c = c_of(side, x)
                new[side, 0, x] = old(side, 0, x) + c * ((hz - behind(hz, 1)) - (hy - down(hy)))
                new[side, 1, x] = old(side, 1, x) + c * ((hx - down(hx)) - (hz - new[side, 5, x - 1]))
                new[side, 2, x] = old(side, 2, x) + c * ((hy - new[side, 4, x - 1]) - (hx - behind(hx, 0)))

    tile = (pl.ds(0, 8), pl.ds(NY - 8, 8))

    def from_block(side, k, x):
        return F[k, x, tile[side], :]

    def from_strip(side, k, x):
        return T[side, k, x]

    def closed_ahead(side, x):
        return lambda v, _: jnp.where(sub < 7, pltpu.roll(v, 7, 0), 0.0)

    def closed_behind(side, x):
        return lambda v, _: jnp.where(sub > 0, pltpu.roll(v, 1, 0), 0.0)

    for step in range(ITERS):
        step_strips(
            step, from_block if step == 0 else from_strip, T,
            lambda side, x: from_block(side, 6, x), closed_ahead, closed_behind,
        )
        for x in range(step, WIDE - 1 - step):
            row = pl.ds(x + 4, 1)
            SB[6 + step, 0, row] = T[1, 3, x, pl.ds(7, 1), :]
            SB[6 + step, 1, row] = T[1, 5, x, pl.ds(7, 1), :]
        post(6 + step)
        if step < ITERS - 1:
            for x in range(step + 1, WIDE - 1 - step):
                row = pl.ds(x + 4, 1)
                SB[3 + step, 0, row] = T[0, 0, x, pl.ds(0, 1), :]
                SB[3 + step, 1, row] = T[0, 2, x, pl.ds(0, 1), :]
            post(3 + step)

    border_arrives((2,))
    each_border((0, 1, 2), lambda copy, _: copy.wait_send())
    loads[2].wait()
    for load in loads[3:]:
        load.wait()

    def next_y(v):
        return jnp.where(iy < NY - 1, pltpu.roll(v, NY - 1, 0), 0.0)

    def last_y(v):
        return jnp.where(iy > 0, pltpu.roll(v, 1, 0), 0.0)

    def next_z(v):
        return jnp.where(iz < NZ - 1, pltpu.roll(v, NZ - 1, 1), 0.0)

    def last_z(v):
        return jnp.where(iz > 0, pltpu.roll(v, 1, 1), 0.0)

    def magnetic(x):
        s = half(x)
        ex, ey, ez = F[0, x], F[1, x], F[2, x]
        return (
            F[3, x] - s * ((next_y(ez) - ez) - (next_z(ey) - ey)),
            F[4, x] - s * ((next_z(ex) - ex) - (F[2, x + 1] - ez)),
            F[5, x] - s * ((F[1, x + 1] - ey) - (next_y(ex) - ex)),
        )

    def electric(x):
        hx, hy, hz = F[3, x], F[4, x], F[5, x]
        c = F[6, x]
        return (
            F[0, x] + c * ((hz - last_y(hz)) - (hy - last_z(hy))),
            F[1, x] + c * ((hx - last_z(hx)) - (hz - F[5, x - 1])),
            F[2, x] + c * ((hy - F[4, x - 1]) - (hx - last_y(hx))),
        )

    def rows_of(first, trips, group, compute, base):
        @pl.loop(0, trips)
        def _(i):
            rows = [first + group * i + j for j in range(group)]
            values = [compute(x) for x in rows]
            for x, value in zip(rows, values):
                for k in range(3):
                    F[base + k, x] = value[k]

    G[...] = jnp.zeros(G.shape, F32)

    @pl.loop(0, ITERS)
    def _(t):
        rows_of(0, 5, 3, magnetic, 3)
        rows_of(1, 7, 2, electric, 0)

        @pl.loop(0, ROWS // 2)
        def _(i):
            for r in (2 * i, 2 * i + 1):
                x = r + EDGE
                G[r] = G[r] + (
                    FE[t, 0, r].astype(F32) * F[0, x] + FE[t, 1, r].astype(F32) * F[1, x]
                    + FE[t, 2, r].astype(F32) * F[2, x]
                )

    for k in range(6):
        for side in range(2):
            D[side, k] = jnp.zeros((WIDE, 8, NZ), F32)

    lower = sub < 4

    def gather(W, direct, z_send, z_recv, p_send, p_recv):
        def slot(s):
            return W.at[pl.ds(ROWS * s, ROWS)]

        def relay(way, k):
            sign = -1 if way == 0 else 1
            return pltpu.make_async_remote_copy(
                src_ref=slot(8 if direct else 8 + sign * 2 * (k - 1)), dst_ref=slot(8 + sign * 2 * k),
                send_sem=z_send.at[way, k - 1], recv_sem=z_recv.at[way, k - 1],
                device_id={"gx": gx - 2 * sign * (k if direct else 1)}, device_id_type=MESH,
            )

        exists = chip_at

        def relays(way, k):
            if direct:
                return chip_at(1 - way, k)
            onward = chip_at(1 - way, 1)
            return onward if k == 1 else onward & exists(way, k - 1)

        def across(way, k):
            sign = -1 if way == 0 else 1
            s = 8 + sign * 2 * k
            i = s // 2 - 1 + core
            return pltpu.make_async_remote_copy(
                src_ref=slot(s), dst_ref=slot(2 * i + 1),
                send_sem=p_send.at[s // 2], recv_sem=p_recv.at[i],
                device_id={"gx": gx + 1 - 2 * core}, device_id_type=MESH,
            )

        def crosses(way, k):
            if k == 0:
                return None
            known = exists(way, k)
            if k == CHIPS:
                known = known & (core == 1 if way == 0 else core == 0)
            return known

        def begin():
            for k in range(CHIPS if direct else 1, 0, -1):
                for way in (0, 1):
                    pl.when(relays(way, k))(functools.partial(lambda w, j: relay(w, j).start(), way, k))
            across(0, 0).start()

        def step(k):
            for way in (0, 1):
                pl.when(exists(way, k))(functools.partial(lambda w: relay(w, k).wait_recv(), way))
                if k < CHIPS and not direct:
                    pl.when(relays(way, k + 1))(functools.partial(lambda w: relay(w, k + 1).start(), way))
                pl.when(crosses(way, k))(functools.partial(lambda w: across(w, k).start(), way))

        def finish():
            for i in range(8):
                other = gx + 2 * i + 1 - 8
                copy = pltpu.make_async_remote_copy(
                    src_ref=slot(2 * i + 1), dst_ref=slot(2 * i + 1),
                    send_sem=p_send.at[0], recv_sem=p_recv.at[i],
                    device_id={"gx": gx + 1 - 2 * core}, device_id_type=MESH,
                )
                pl.when((other >= 0) & (other < nx))(copy.wait_recv)

        def drain():
            across(0, 0).wait_send()
            for k in range(1, CHIPS + 1):
                for way in (0, 1):
                    pl.when(relays(way, k))(functools.partial(lambda w, j: relay(w, j).wait_send(), way, k))
                    pl.when(crosses(way, k))(functools.partial(lambda w, j: across(w, j).wait_send(), way, k))

        return begin, step, finish, drain

    begin_a, step_a, finish_a, drain_a = gather(WA, False, za_send, za_recv, pa_send, pa_recv)
    begin_b, step_b, finish_b, drain_b = gather(WB, False, zb_send, zb_recv, pb_send, pb_recv)

    @pl.loop(0, ROWS)
    def _(r):
        m = G[r] * MV[r].astype(F32)
        WA[8 * ROWS + r, pl.ds(0, 16), :] = m[8:24]
        WA[8 * ROWS + r, pl.ds(16, 8), :] = jnp.where(lower, m[24:32], m[0:8])


    def forward(m, way):
        tile = 2 if way == 0 else 0
        where = {"gx": gx - 1} if way == 0 else {"gx": gx + 1}
        return pltpu.make_async_remote_copy(
            src_ref=RB.at[m, :, middle], dst_ref=RB.at[m, :, pl.ds(8 * tile, 8)],
            send_sem=fwd_send.at[m, way], recv_sem=fwd_recv.at[m, way], device_id=where, device_id_type=MESH,
        )

    begin_a()
    order = (0, 1, 2, 6, 3, 7, 4, 8, 5, 9)
    for m in order:
        pl.when(receives(m))(functools.partial(lambda i: far(i).wait_recv(), m))
        pl.when(receives(m) & has_left)(functools.partial(lambda i: forward(i, 0).start(), m))
        pl.when(receives(m) & has_right)(functools.partial(lambda i: forward(i, 1).start(), m))

    def arrived(m):
        pl.when(receives(m) & has_right)(functools.partial(lambda i: forward(i, 0).wait_recv(), m))
        pl.when(receives(m) & has_left)(functools.partial(lambda i: forward(i, 1).wait_recv(), m))

    for m in order:
        arrived(m)

    @pl.loop(0, WIDE)
    def _(x):
        row = pl.ds(x + 4, 1)
        c = F[6, x]
        near, next_near = RB[1, 0, row], RB[1, 1, row]
        CS[0, x] = jnp.where(lower, c[0:8], jnp.where(sub == 7, near, jnp.where(sub == 6, next_near, 0.0)))
        near, next_near = RB[0, 0, row], RB[0, 1, row]
        CS[1, x] = jnp.where(lower, jnp.where(sub == 0, near, jnp.where(sub == 1, next_near, 0.0)), c[24:32])

    inflow = jnp.where(has_below, 1.0, 0.0).astype(F32)

    def strip(side, k, x):
        return D[side, k, x]

    def open_ahead(step):
        def ahead_at(side, x):
            planes, row = (SB if side == 0 else RB), pl.ds(x + 4, 1)

            def ahead(v, comp):
                trace = planes[2 + step, comp, row]
                trace = trace * inflow if side == 0 else trace
                return pltpu.roll(v, 7, 0) + jnp.where(sub == 7, trace, 0.0)

            return ahead

        return ahead_at

    def open_behind(step):
        def behind_at(side, x):
            planes, row = (RB if side == 0 else SB), pl.ds(x + 4, 1)
            return lambda v, comp: pltpu.roll(v, 1, 0) + jnp.where(sub == 0, planes[6 + step, comp, row], 0.0)

        return behind_at

    half_tile = (pl.ds(0, 16), pl.ds(NY - 16, 16))
    for step in range(ITERS):
        step_strips(step, strip, D, lambda side, x: CS[side, x], open_ahead(step), open_behind(step))
        for r in range(ROWS):
            for side in range(2):
                stored = [FE[step, k, r, half_tile[side], :].astype(F32) for k in range(3)]
                stored = [v[0:8] if side == 0 else v[8:16] for v in stored]
                e = [D[side, k, r + EDGE] for k in range(3)]
                g = stored[0] * e[0] + stored[1] * e[1] + stored[2] * e[2]
                GS[side, r] = g if step == 0 else GS[side, r] + g

    @pl.loop(0, ROWS)
    def _(r):
        g = jnp.where(lower, G[r, pl.ds(0, 8), :] + GS[0, r], G[r, pl.ds(24, 8), :] + GS[1, r])
        mask = jnp.where(lower, MV[r, pl.ds(0, 8), :], MV[r, pl.ds(24, 8), :])
        WB[8 * ROWS + r] = g * mask.astype(F32)

    step_a(1)
    begin_b()

    @pl.loop(0, ROWS)
    def _(r):
        x = r + EDGE
        for k in range(3):
            e = F[k, x]
            final_ref[k, r, pl.ds(8, 16), :] = e[8:24]
            final_ref[k, r, pl.ds(0, 8), :] = e[0:8] + jnp.where(lower, D[0, k, x], 0.0)
            final_ref[k, r, pl.ds(24, 8), :] = e[24:32] + jnp.where(lower, 0.0, D[1, k, x])

    for k in range(1, CHIPS + 1):
        if k > 1:
            step_a(k)
        step_b(k)
    finish_a()
    finish_b()

    taps = [tap_ref[b] for b in range(BAND)]
    starts = [off_ref[b] + REACH for b in range(BAND)]

    @pl.loop(0, ROWS)
    def _(r):
        wide, thin = taps[0] * WA[starts[0] + r], taps[0] * WB[starts[0] + r]
        for b in range(1, BAND):
            wide = wide + taps[b] * WA[starts[b] + r]
            thin = thin + taps[b] * WB[starts[b] + r]
        mixed = wide[16:24]
        filt_ref[r, pl.ds(8, 16), :] = wide[0:16]
        filt_ref[r, pl.ds(0, 8), :] = jnp.where(lower, thin, mixed)
        filt_ref[r, pl.ds(24, 8), :] = jnp.where(lower, mixed, thin)

    for m in range(MESSAGES):
        pl.when(sends(m))(functools.partial(lambda i: far(i).wait_send(), m))
        pl.when(receives(m) & has_left)(functools.partial(lambda i: forward(i, 0).wait_send(), m))
        pl.when(receives(m) & has_right)(functools.partial(lambda i: forward(i, 1).wait_send(), m))
    drain_a()
    drain_b()


def solution(mesh):
    nx, ny = mesh.shape["gx"], mesh.shape["gy"]

    def shards(*arguments):
        dma = pltpu.SemaphoreType.DMA
        hbm, vmem = (pl.BlockSpec(memory_space=s) for s in (pltpu.HBM, pltpu.VMEM))
        return pl.pallas_call(
            functools.partial(kernel, nx, ny),
            out_shape=(
                jax.ShapeDtypeStruct((ROWS, NY, NZ), F32),
                jax.ShapeDtypeStruct((3, ROWS, NY, NZ), F32),
            ),
            in_specs=[hbm] * 6,
            out_specs=(vmem, vmem),
            scratch_shapes=[
                pltpu.VMEM((7, WIDE, NY, NZ), F32),
                pltpu.VMEM((ITERS, 3, ROWS, NY, NZ), jnp.bfloat16),
                pltpu.VMEM((ROWS, NY, NZ), F32),
                pltpu.VMEM((ROWS, NY, NZ), jnp.int32),
                pltpu.VMEM((ROWS, NY, NZ), F32),
                pltpu.VMEM((MESSAGES, 2, 24, NZ), F32),
                pltpu.VMEM((MESSAGES, 2, 24, NZ), F32),
                pltpu.VMEM((2, 6, WIDE, 8, NZ), F32),
                pltpu.VMEM((2, 6, WIDE, 8, NZ), F32),
                pltpu.VMEM((2, WIDE, 8, NZ), F32),
                pltpu.VMEM((2, ROWS, 8, NZ), F32),
                pltpu.VMEM((17 * ROWS, 24, NZ), F32),
                pltpu.VMEM((17 * ROWS, 8, NZ), F32),
                pltpu.SMEM((BAND,), jnp.int32), pltpu.SMEM((BAND,), F32),
                dma((6,)), dma((2, 3)), dma((2, 3)),
                dma((MESSAGES,)), dma((MESSAGES,)), dma((MESSAGES, 2)), dma((MESSAGES, 2)),
                dma((2, CHIPS)), dma((2, CHIPS)), dma((9,)), dma((8,)),
                dma((2, CHIPS)), dma((2, CHIPS)), dma((9,)), dma((8,)),
            ],
            compiler_params=pltpu.CompilerParams(collective_id=0, has_side_effects=True, vmem_limit_bytes=16 << 20),
            name="adjoint_yee_filter",
        )(
            *(pltpu.with_memory_space_constraint(a, pltpu.HBM) for a in arguments),
        )

    return jax.shard_map(
        shards,
        mesh=mesh,
        in_specs=(
            P(None, "gx", "gy", None),
            P(None, None, "gx", "gy", None),
            P("gx", "gy", None),
            P("gx", "gy", None),
            P(),
            P(),
        ),
        out_specs=(P("gx", "gy", None), P(None, "gx", "gy", None)),
        check_vma=False,
    )
```
